32 devices in a mesh: leaf: 16 (over z, y, x), sub: 2 (over core).
Axes of the slice: x: 2, y: 2, z: 4, core: 2. Of those that a mesh axis runs over, the one named last changes fastest.
Arguments:
- probes: float32 [64, 32768], P(None, ('leaf', 'sub')), may hold values from -600 to 600
- points: float32 [3, 32768], P(None, ('leaf', 'sub')), may hold values from -4 to 4
- leaf_order: int32 [32768], P(('leaf', 'sub')), may hold values from 0 to 1023, as said below
- near_list: int32 [64, 4], P(('leaf', 'sub')), may hold values from 0 to 63, as said below
- far_leaf_list: int32 [64, 2], P(('leaf', 'sub')), may hold values from 0 to 63, as said below
- far_chip_list: int32 [16, 8], P('leaf'), may hold values from -1 to 15, as said below
- leaf_basis: float32 [64, 512, 256], P(('leaf', 'sub')), may hold values from -0.25 to 0.25
- transfer: float32 [64, 256, 256], P(('leaf', 'sub')), may hold values from -0.1875 to 0.1875
- far_leaf_blocks: float32 [128, 256, 256], P(('leaf', 'sub')), may hold values from -0.25 to 0.25
- far_chip_blocks: float32 [128, 256, 256], P('leaf'), may hold values from -0.125 to 0.125
Outputs:
- result: float32 [64, 32768], P(None, ('leaf', 'sub'))
The draws below stay inside these ranges and needn't reach their ends.
Inputs may be any that keep to these rules, and one draw needn't show every extreme that they name: `leaf_order`: each device's block of 1024 consecutive entries is a permutation of 0 to 1023. `near_list`: row l lists 4 distinct leaves, l among them, all held by the devices l // 2 - 1 to l // 2 + 1 of the joined axis leaf+sub, counted around the cycle. `far_leaf_list`: row l lists the 2 leaves of those same three devices that row l of near_list leaves out. `far_chip_list`: row k lists distinct chip clusters at cycle distance 2 to 5 from k, one to 8 of them, the used entries first and -1 in the rest; some row uses all 8.
All inputs are finite; a program needn't handle non-finite values.
Results may differ from the reference program's by a relative error of at most 0.0003.
Values sent between devices are 32-bit elements; how exact they have to be, the bound alone decides.
No kernel may reach another device: no remote copies, remote signals or barrier semaphores. Data moves between devices by JAX's collectives and lax.ppermute only.
A program may use at most 64 MiB of HBM per device.

```python
import math
import jax
import jax.numpy as jnp
from jax import lax

LEAF = 512
RANK = 256
COLS = 64
LD = 2
CHIP_SPAN = 4
NEAR = 4
FARL = 2
FARC = 8
PTS_DEV = 1024
LEAVES = 64
CHIPS = 16
CHIP_LEAVES = 4
POINTS = 32768
DEVICES = 32


def point_layout(key):
    sub_key = jax.random.fold_in(key, 11)
    perm_key, jitter_key = jax.random.split(sub_key)
    device_keys = jax.random.split(perm_key, DEVICES)
    perms = jax.vmap(lambda one_key: jax.random.permutation(one_key, PTS_DEV))(device_keys).astype(jnp.int32)
    leaf_of = (jnp.arange(POINTS) // LEAF).astype(jnp.float32)
    radius = LEAVES / (8.0 * math.pi)
    angle = 2.0 * math.pi * (leaf_of + 0.5) / LEAVES
    centers = jnp.stack([radius * jnp.cos(angle), radius * jnp.sin(angle), jnp.zeros_like(angle)])
    jitter = jax.random.uniform(jitter_key, (3, POINTS), jnp.float32, -0.5, 0.5)
    sorted_points = centers + jitter
    positions = (jnp.arange(DEVICES, dtype=jnp.int32)[:, None] * PTS_DEV + perms).reshape(-1)
    placed = jnp.zeros((3, POINTS), jnp.float32).at[:, positions].set(sorted_points)
    return (perms.reshape(-1), placed)


def draw_leaf_order(key, part):
    return point_layout(key)[0]


def draw_points(key, part):
    return point_layout(key)[1]


def leaf_lists(key):
    sub_key = jax.random.fold_in(key, 23)
    window = 3 * LD
    scores = jax.random.randint(sub_key, (LEAVES, window), 0, 1 << 20) * window + jnp.arange(window)[None, :]
    own_slot = LD + jnp.arange(LEAVES) % LD
    scores = jnp.where(jnp.arange(window)[None, :] == own_slot[:, None], -1, scores)
    ranked = jnp.argsort(scores, axis=1)
    first_leaf = (jnp.arange(LEAVES) // LD - 1) * LD
    leaf_ids = jnp.mod(first_leaf[:, None] + ranked, LEAVES).astype(jnp.int32)
    return (leaf_ids[:, :NEAR], leaf_ids[:, NEAR:])


def draw_near_list(key, part):
    return leaf_lists(key)[0]


def draw_far_leaf_list(key, part):
    return leaf_lists(key)[1]


def draw_far_chip_list(key, part):
    sub_key = jax.random.fold_in(key, 37)
    score_key, count_key, fullest_key = jax.random.split(sub_key, 3)
    width = 2 * CHIP_SPAN
    scores = jax.random.randint(score_key, (CHIPS, width), 0, 1 << 20) * width + jnp.arange(width)[None, :]
    ranked = jnp.argsort(scores, axis=1)
    distance = jnp.where(ranked < CHIP_SPAN, ranked + 2, -(ranked - CHIP_SPAN + 2))
    targets = jnp.mod(jnp.arange(CHIPS)[:, None] + distance, CHIPS)
    counts = jax.random.randint(count_key, (CHIPS,), 1, width + 1)
    fullest = jax.random.randint(fullest_key, (), 0, CHIPS)
    counts = jnp.where(jnp.arange(CHIPS) == fullest, width, counts)
    live = jnp.arange(width)[None, :] < counts[:, None]
    return jnp.where(live, targets, -1).astype(jnp.int32)


def draw_probes(key, part):
    sub_key = jax.random.fold_in(key, 5)
    base_key, row_key, column_key = jax.random.split(sub_key, 3)
    device_of = (jnp.arange(POINTS) // PTS_DEV).astype(jnp.float32)
    rising = 3.0 ** (device_of / max(DEVICES - 1, 1))
    row_scale = jnp.exp(jax.random.uniform(row_key, (POINTS,), jnp.float32, 0.0, math.log(10.0 / 3.0)))
    column_scale = jnp.exp(jax.random.uniform(column_key, (COLS, 1), jnp.float32, 0.0, math.log(10.0)))
    values = jnp.clip(jax.random.normal(base_key, (COLS, POINTS), jnp.float32), -6.0, 6.0)
    return values * column_scale * (rising * row_scale)[None, :]


def shard_levels(rng, dims, shards, least, top_value):
    loudness = 1.0
    for axis_at, parts in shards:
        draws = jax.random.uniform(jax.random.fold_in(jax.random.fold_in(rng, 6), axis_at), (parts,), jnp.float32, least / len(shards), top_value / len(shards))
        loudness = loudness * jnp.repeat(jnp.exp(draws), dims[axis_at] // parts).reshape((-1,) + (1,) * (len(dims) - 1 - axis_at))
    return loudness


def gaussian(rng, extent, scale, reach, shards=(), kind=jnp.bfloat16):
    drawn = jax.random.normal(rng, extent, jnp.float32) * scale
    if len(shards) > 0:
        drawn = shard_levels(rng, extent, shards, -0.22, 0.18) * drawn
    return jnp.clip(drawn, min=-reach, max=reach).astype(kind)


def setup_inputs(seed: int = 0) -> dict:
    streams_of = jax.random.split(jax.random.key(seed), 11)
    return {
        "probes": draw_probes(jax.random.fold_in(streams_of[10], 71), 0),
        "points": draw_points(jax.random.fold_in(streams_of[10], 71), 0),
        "leaf_order": draw_leaf_order(jax.random.fold_in(streams_of[10], 71), 0),
        "near_list": draw_near_list(jax.random.fold_in(streams_of[10], 71), 0),
        "far_leaf_list": draw_far_leaf_list(jax.random.fold_in(streams_of[10], 71), 0),
        "far_chip_list": draw_far_chip_list(jax.random.fold_in(streams_of[10], 71), 0),
        "leaf_basis": gaussian(streams_of[6], (LEAVES, LEAF, RANK), LEAF ** -0.5, 0.25, ((0, 32),), jnp.float32),
        "transfer": gaussian(streams_of[7], (LEAVES, RANK, RANK), (CHIP_LEAVES * RANK) ** -0.5, 0.1875, ((0, 32),), jnp.float32),
        "far_leaf_blocks": gaussian(streams_of[8], (LEAVES * FARL, RANK, RANK), (FARL * RANK) ** -0.5, 0.25, ((0, 32),), jnp.float32),
        "far_chip_blocks": gaussian(streams_of[9], (CHIPS * FARC, RANK, RANK), (FARC * RANK) ** -0.5, 0.125, ((0, 16),), jnp.float32),
    }


highest = lax.Precision.HIGHEST
inverse_width = 0.5 / (0.15 * 0.15)
epsilon = 1e-06

def kernel_tiles(source_points, target_points):
    spread = source_points[0] - target_points[0]
    distance = spread * spread
    for coord_axis in (1, 2):
        spread = source_points[coord_axis] - target_points[coord_axis]
        distance = distance + spread * spread
    return jnp.exp(-inverse_width * distance)

def apply_matrix(sorted_values, point_tiles, near_list, far_leaf_list, far_chip_list, leaf_basis, transfer, far_leaf_blocks, far_chip_blocks):
    value_tiles = sorted_values.reshape(COLS, LEAVES, LEAF)

    def one_leaf(leaf_id):
        sources = near_list[leaf_id]
        source_points = point_tiles[:, sources]
        target_points = point_tiles[:, leaf_id]
        kernels = kernel_tiles(source_points[..., :, None], target_points[:, None, None, :])
        source_values = value_tiles[:, sources]
        return jnp.einsum('cnp,npq->cq', source_values, kernels, precision=highest)
    near_part = lax.map(one_leaf, jnp.arange(LEAVES, dtype=jnp.int32))
    coefficients = jnp.einsum('clp,lpr->lcr', value_tiles, leaf_basis, precision=highest)
    far_sources = coefficients[far_leaf_list]
    leaf_blocks = far_leaf_blocks.reshape(LEAVES, FARL, RANK, RANK)
    local_far = jnp.einsum('ljcr,ljrs->lcs', far_sources, leaf_blocks, precision=highest)
    upward = jnp.einsum('lcr,lrs->lcs', coefficients, transfer, precision=highest)
    chip_coeffs = lax.optimization_barrier(jnp.sum(upward.reshape(CHIPS, CHIP_LEAVES, COLS, RANK), axis=1))
    valid = far_chip_list >= 0
    safe_ids = jnp.where(valid, far_chip_list, 0)
    chip_sources = chip_coeffs[safe_ids] * valid[:, :, None, None].astype(jnp.float32)
    chip_blocks = far_chip_blocks.reshape(CHIPS, FARC, RANK, RANK)
    chip_far = jnp.einsum('kjcr,kjrs->kcs', chip_sources, chip_blocks, precision=highest)
    per_leaf = jnp.repeat(chip_far, CHIP_LEAVES, axis=0)
    downward = local_far + jnp.einsum('lcs,lrs->lcr', per_leaf, transfer, precision=highest)
    far_part = jnp.einsum('lcr,lpr->lcp', downward, leaf_basis, precision=highest)
    summed_part = near_part + far_part
    return jnp.transpose(summed_part, (1, 0, 2)).reshape(COLS, POINTS)

def reference(probes, points, leaf_order, near_list, far_leaf_list, far_chip_list, leaf_basis, transfer, far_leaf_blocks, far_chip_blocks):
    block_start = jnp.arange(POINTS, dtype=jnp.int32) // PTS_DEV * PTS_DEV
    source_index = (block_start + leaf_order).astype(jnp.int32)
    sorted_probes = probes[:, source_index]
    sorted_points = points[:, source_index]
    point_tiles = sorted_points.reshape(3, LEAVES, LEAF)
    first_pass = apply_matrix(sorted_probes, point_tiles, near_list, far_leaf_list, far_chip_list, leaf_basis, transfer, far_leaf_blocks, far_chip_blocks)
    squares = lax.optimization_barrier(jnp.sum(first_pass * first_pass, axis=1))
    column_scale = lax.rsqrt(squares / POINTS + epsilon)
    second = apply_matrix(first_pass * column_scale[:, None], point_tiles, near_list, far_leaf_list, far_chip_list, leaf_basis, transfer, far_leaf_blocks, far_chip_blocks)
    return jnp.zeros_like(second).at[:, source_index].set(second)
```

```python
import functools

import jax
import jax.numpy as jnp
from jax import lax
from jax.experimental import pallas as pl
from jax.experimental.pallas import tpu as pltpu
from jax.sharding import PartitionSpec as P

CHIP_SPAN = 4
WIDTH = 0.15
epsilon = 1e-06
JOINED = ("leaf", "sub")

f32 = jnp.float32
bf16 = jnp.bfloat16
VM = pl.BlockSpec(memory_space=pltpu.VMEM)
SM = pl.BlockSpec(memory_space=pltpu.SMEM)
NN = (((1,), (0,)), ((), ()))
NT = (((1,), (1,)), ((), ()))


def halves(x):
    high = x.astype(bf16)
    return high, (x - high.astype(f32)).astype(bf16)


def dot(a, b, dims=NN):
    return lax.dot_general(a, b, dims, preferred_element_type=f32)


def product(pair, weights, dims=NN):
    high, low = pair
    w_high, w_low = weights
    rows = high.shape[0]
    both = dot(jnp.concatenate([high, low], 0), w_high, dims)
    return both[:rows] + both[rows:] + dot(high, w_low, dims)


def sort_kernel(probes, points, order, basis, transfer, packed, upward):
    leaves, size, rank = basis.shape
    count = probes.shape[1]
    rows = probes.shape[0]
    chunk = 256
    high, low = halves(probes[...])
    three = points[...]
    dims = three.shape[0]
    three = jnp.concatenate([three, jnp.zeros((8 - dims, count), f32)], 0)
    p1 = three.astype(bf16)
    rest = three - p1.astype(f32)
    p2, p3 = halves(rest)
    left = jnp.concatenate([high, low, jnp.concatenate([p1.astype(f32), p2.astype(f32), p3.astype(f32), jnp.zeros((8, count), f32)], 0).astype(bf16)], 0)
    places = order[...]
    total = jnp.zeros((left.shape[0], count), f32)
    for start in range(0, count, chunk):
        spots = lax.broadcasted_iota(jnp.int32, (chunk, count), 0) + start
        pick = jnp.where(spots == places, 1.0, 0.0).astype(bf16)
        total = total + dot(left[:, start : start + chunk], pick)
    packed[:rows, :count] = total[:rows] + total[rows : 2 * rows]
    base = 2 * rows
    packed[rows : rows + 8, :count] = total[base : base + 8] + total[base + 8 : base + 16] + total[base + 16 : base + 24]
    packed[rows : rows + 8, count:] = jnp.zeros((8, leaves * rank), f32)
    v_high = total[:rows].astype(bf16)
    v_low = total[rows : 2 * rows].astype(bf16)
    up = jnp.zeros((rows, rank), f32)
    for leaf in range(leaves):
        cut = slice(leaf * size, (leaf + 1) * size)
        coeff = product((v_high[:, cut], v_low[:, cut]), halves(basis[leaf]))
        packed[:rows, count + leaf * rank : count + (leaf + 1) * rank] = coeff
        up = up + product(halves(coeff), halves(transfer[leaf]))
    upward[...] = up


def near_kernel(blocks, first, ready, scale, near_list, far_list, meta, *refs):
    refs = list(refs)
    own = refs.pop(0)
    sources = [own if b == 0 else refs.pop(0) for b in blocks]
    far_blocks = refs.pop(0)
    if not first:
        near_in, e_in = refs.pop(0), refs.pop(0)
    if ready:
        k_high, k_low = refs.pop(0), refs.pop(0)
    near_out, e_out = refs.pop(0), refs.pop(0)
    if not ready:
        k_high, k_low, columns = refs.pop(0), refs.pop(0), refs.pop(0)
    rows = near_out.shape[0]
    count = near_out.shape[1]
    leaves = near_list.shape[0]
    size = count // leaves
    rank = far_blocks.shape[1]
    if first:
        near_out[...] = jnp.zeros(near_out.shape, f32)
        e_out[...] = jnp.zeros(e_out.shape, f32)
    else:
        near_out[...] = near_in[...]
        e_out[...] = e_in[...]
    if not ready:
        targets = own[rows : rows + 8, :count] * scale
    for at, (block, source) in enumerate(zip(blocks, sources)):
        if not ready:
            turned = jnp.transpose(source[rows : rows + 8, :count] * scale)
            for axis in range(3):
                columns[axis] = jnp.broadcast_to(turned[:, axis : axis + 1], (count, 128))
        for inner in range(leaves):
            leaf_id = meta[block] + inner
            cut = slice(inner * size, (inner + 1) * size)
            for target in range(leaves):
                is_near = leaf_id == near_list[target, 0]
                for slot in range(1, near_list.shape[1]):
                    is_near = jnp.logical_or(is_near, leaf_id == near_list[target, slot])
                out = slice(target * size, (target + 1) * size)
                tile = (at * leaves + inner) * leaves + target

                @pl.when(is_near)
                def _():
                    if not ready:
                        step = 64
                        for start in range(0, size, step):
                            distance = None
                            for axis in range(3):
                                piece = columns[axis, inner * size + start : inner * size + start + step]
                                spread = jnp.concatenate([piece] * (size // 128), 1) - targets[axis : axis + 1, out]
                                square = spread * spread
                                distance = square if distance is None else distance + square
                            k = jnp.exp(-distance)
                            high, low = halves(k)
                            k_high[tile, start : start + step] = high
                            k_low[tile, start : start + step] = low
                    values = halves(source[:rows, cut])
                    near_out[:, out] += product(values, (k_high[tile], k_low[tile]))

                @pl.when(jnp.logical_not(is_near))
                def _():
                    slot = 0
                    for j in range(1, far_list.shape[1]):
                        slot = jnp.where(leaf_id == far_list[target, j], j, slot)
                    coeff = source[:rows, count + inner * rank : count + (inner + 1) * rank]
                    weights = far_blocks[target * far_list.shape[1] + slot]
                    e_out[:, target * rank : (target + 1) * rank] += product(halves(coeff), halves(weights))


def couple_kernel(far_chip_list, meta, *refs):
    *arrived, blocks, out = refs
    out[...] = jnp.zeros(out.shape, f32)
    for at, source in enumerate(arrived):
        chip = meta[3 + at]
        slot = jnp.int32(-1)
        for j in range(far_chip_list.shape[1]):
            slot = jnp.where(far_chip_list[0, j] == chip, j, slot)

        @pl.when(slot >= 0)
        def _():
            out[...] += product(halves(source[...]), halves(blocks[slot]))


def downward(h_own, h_other, near, e, basis, transfer):
    leaves, size, rank = basis.shape
    h = halves(h_own[...] + h_other[...])
    for leaf in range(leaves):
        weights = halves(basis[leaf])
        t = halves(transfer[leaf])
        cut = slice(leaf * rank, (leaf + 1) * rank)
        down = e[:, cut] + product(h, t, NT)
        yield leaf, near[:, leaf * size : (leaf + 1) * size] + product(halves(down), weights, NT), weights, t


def turn_kernel(h_own, h_other, near, e, basis, transfer, packed, upward, squares):
    leaves, size, rank = basis.shape
    rows, count = near.shape
    up = jnp.zeros((rows, rank), f32)
    total = jnp.zeros((rows, 1), f32)
    for leaf, value, weights, t in downward(h_own, h_other, near, e, basis, transfer):
        packed[:, leaf * size : (leaf + 1) * size] = value
        coeff = product(halves(value), weights)
        packed[:, count + leaf * rank : count + (leaf + 1) * rank] = coeff
        up = up + product(halves(coeff), t)
        total = total + jnp.sum(value * value, axis=1, keepdims=True)
    upward[...] = up
    squares[...] = jnp.broadcast_to(total, squares.shape)


def last_kernel(points_total, h_own, h_other, near, e, basis, transfer, order, squares, result):
    leaves, size, rank = basis.shape
    rows, count = near.shape
    scale = lax.rsqrt(squares[:, :1] / points_total + epsilon)
    parts = []
    for leaf, value, _, _ in downward(h_own, h_other, near, e, basis, transfer):
        parts.append(value * scale)
    high, low = halves(jnp.concatenate(parts, 1))
    left = jnp.concatenate([high, low], 0)
    places = order[...]
    chunk = 256
    for start in range(0, count, chunk):
        spots = lax.broadcasted_iota(jnp.int32, (chunk, count), 0) + start
        pick = jnp.where(spots == places, 1.0, 0.0).astype(bf16)
        moved = dot(left, pick, NT)
        result[:, start : start + chunk] = moved[:rows] + moved[rows:]


def call(kernel, outs, specs, args, name, scratch=(), vmem=24):
    return pl.pallas_call(
        kernel,
        out_shape=outs,
        in_specs=specs,
        out_specs=[VM] * len(outs),
        scratch_shapes=list(scratch),
        name=name,
        compiler_params=pltpu.CompilerParams(vmem_limit_bytes=vmem << 20),
    )(*args)


def shape(*dims, dtype=f32):
    return jax.ShapeDtypeStruct(dims, dtype)


def on_device(probes, points, leaf_order, near_list, far_leaf_list, far_chip_list, leaf_basis, transfer, far_leaf_blocks, far_chip_blocks):
    leaves, size, rank = leaf_basis.shape
    rows, count = probes.shape
    chips = lax.axis_size("leaf")
    devices = lax.axis_size(JOINED)
    points_total = count * devices
    assert lax.axis_size("sub") == 2 and chips > 2 * (CHIP_SPAN + 1)

    def place(chip, core):
        return chip % chips * 2 + core

    across = [(place(k, s), place(k, 1 - s)) for k in range(chips) for s in (0, 1)]
    beside = [(place(k, 1), place(k + 1, 0)) for k in range(chips)]
    beside = beside + [(b, a) for a, b in beside]
    distances = range(2, CHIP_SPAN + 2)
    routes = [[(place(k, 0), place(k + d, 0)) for k in range(chips)] + [(place(k, 1), place(k - d, 1)) for k in range(chips)] for d in distances]

    device = lax.axis_index(JOINED)
    core = lax.axis_index("sub")
    chip = lax.axis_index("leaf")
    other = device + 1 - 2 * core
    off = jnp.mod(device - 1 + 2 * core, devices)
    at = jnp.arange(8)
    step = jnp.where(core == 0, -1, 1)
    far_chip = jnp.mod(chip + step * (at - 1), chips)
    meta = jnp.where(at == 0, device * leaves, jnp.where(at == 1, other * leaves, jnp.where(at == 2, off * leaves, far_chip))).astype(jnp.int32)

    order = leaf_order.reshape(1, count)
    packed, upward = call(
        sort_kernel,
        [shape(rows + 8, count + leaves * rank), shape(rows, rank)],
        [VM] * 5,
        (probes, points, order, leaf_basis, transfer),
        "sort",
    )
    scale = (0.5 ** 0.5) / WIDTH
    kernels = {}

    def near_terms(blocks, sources, before, key):
        ready = key in kernels
        tiles = len(blocks) * leaves * leaves
        args = [near_list, far_leaf_list, meta, *sources, far_leaf_blocks]
        specs = [SM] * 3 + [VM] * (len(sources) + 1)
        if before is not None:
            args += list(before)
            specs += [VM] * 2
        outs = [shape(rows, count), shape(rows, leaves * rank)]
        scratch = []
        if ready:
            args += list(kernels[key])
            specs += [VM] * 2
        else:
            outs += [shape(tiles, size, size, dtype=bf16)] * 2
            scratch = [pltpu.VMEM((3, count, 128), f32)]
        body = functools.partial(near_kernel, blocks, before is None, ready, scale)
        found = call(body, outs, specs, args, key + ("_again" if ready else ""), scratch)
        if not ready:
            kernels[key] = found[2:]
        return found[:2]

    def product_terms(packed, upward):
        other_up = lax.ppermute(upward, JOINED, across)
        both = upward + other_up
        arrived = [lax.ppermute(both, JOINED, route) for route in routes]
        packed_other = lax.ppermute(packed, JOINED, across)
        packed_off = lax.ppermute(packed, JOINED, beside)
        terms = near_terms((0, 1), (packed, packed_other), None, "near_chip")
        (coupled,) = call(
            couple_kernel,
            [shape(rows, rank)],
            [SM] * 2 + [VM] * (len(arrived) + 1),
            (far_chip_list, meta, *arrived, far_chip_blocks),
            "couple",
        )
        coupled_other = lax.ppermute(coupled, JOINED, across)
        near, e = near_terms((2,), (packed, packed_off), terms, "near_beside")
        return coupled, coupled_other, near, e

    found = product_terms(packed, upward)
    packed, upward, squares = call(
        turn_kernel,
        [shape(rows, count + leaves * rank), shape(rows, rank), shape(rows, 128)],
        [VM] * 6,
        (*found, leaf_basis, transfer),
        "turn",
    )
    bit = 1
    while bit < devices:
        squares = squares + lax.ppermute(squares, JOINED, [(i, i ^ bit) for i in range(devices)])
        bit *= 2
    found = product_terms(packed, upward)
    (result,) = call(
        functools.partial(last_kernel, points_total),
        [shape(rows, count)],
        [VM] * 8,
        (*found, leaf_basis, transfer, order, squares),
        "last",
    )
    return result


def solution(mesh):
    return jax.shard_map(
        on_device,
        mesh=mesh,
        in_specs=(
            P(None, JOINED),
            P(None, JOINED),
            P(JOINED),
            P(JOINED, None),
            P(JOINED, None),
            P("leaf", None),
            P(JOINED, None, None),
            P(JOINED, None, None),
            P(JOINED, None, None),
            P("leaf", None, None),
        ),
        out_specs=P(None, JOINED),
        check_vma=False,
    )
```
